32 devices in a mesh: line: 4 (over z), tx: 2 (over core), ty: 4 (over y, x).
Axes of the slice: x: 2, y: 2, z: 4, core: 2. Of those that a mesh axis runs over, the one named last changes fastest.
Arguments:
- right_side: float32 [16, 8, 16, 128], P('line', 'tx', 'ty'), may hold values from -3 to 3
- start_field: float32 [16, 8, 16, 128], P('line', 'tx', 'ty'), may hold values from -3 to 3
- line_inverse: bfloat16 [16, 8, 16, 128, 128], P('line', 'tx', 'ty'), as said below
- lower_scale: float32 [16, 8, 16], P('line', 'tx', 'ty'), may hold values from 0.85 to 1
- upper_scale: float32 [16, 8, 16], P('line', 'tx', 'ty'), may hold values from 0.85 to 1
- lower_block: float32 [128, 128], replicated
- upper_block: float32 [128, 128], replicated
- face_blocks: float32 [4, 128, 128], replicated, may hold values from -0.15625 to 0.15625
- face_kind: int32 [4, 16, 8, 16], P(None, 'line', 'tx', 'ty'), may hold values from 0 to 3
- face_scale: float32 [4, 16, 8, 16], P(None, 'line', 'tx', 'ty'), may hold values from 0.25 to 1
- agglomerate: int32 [16, 8, 16], P('line', 'tx', 'ty'), may hold values from 0 to 63
- restriction: float32 [32, 128], replicated, may hold values from -0.5 to 0.5
- coarse_inverse: float32 [4, 2, 64, 32, 32], P('line', 'tx', 'ty'), as said below
Outputs:
- corrected: float32 [16, 8, 16, 128], P('line', 'tx', 'ty')
- residual: float32 [16, 8, 16, 128], P('line', 'tx', 'ty')
The draws below stay inside these ranges and needn't reach their ends.
Inputs may be any that keep to these rules, and one draw needn't show every extreme that they name: An element's agglomerate is one of the 64 agglomerates of its own column. `line_inverse`: each block is a diagonal of positive entries plus a full-rank part. `coarse_inverse`: each block is a diagonal of positive entries plus a full-rank part.
All inputs are finite; a program needn't handle non-finite values.
Results may differ from the reference program's by a relative error of at most 0.0003.
Values sent between devices are 32-bit elements; how exact they have to be, the bound alone decides.
A program may use at most 64 MiB of HBM per device.

```python
import math
import jax
import jax.numpy as jnp
from jax import lax

B = 128
CB = 32
SWEEPS = 2
SEG = 4
LX = 4
LINES = 16
NX = 8
NY = 16
NAGG = 64
N_LINE = 4
N_TX = 2


def draw_line_inverse(key, part):
    slab_keys = jax.random.split(key, LINES)

    def one_slab(slab_key):
        diag_key, jitter_key = jax.random.split(slab_key)
        diagonal = jnp.exp(jax.random.uniform(diag_key, (NX, NY, B), jnp.float32, math.log(0.85), math.log(1.1)))
        jitter = 0.2 * jax.random.normal(jitter_key, (NX, NY, B, B), jnp.float32) * B ** (-0.5)
        return (jitter + diagonal[..., None] * jnp.eye(B, dtype=jnp.float32)).astype(jnp.bfloat16)
    return lax.map(one_slab, slab_keys)


def coupling_block(block_key):
    jitter = 0.2 * jax.random.normal(block_key, (B, B), jnp.float32) * B ** (-0.5)
    return jnp.eye(B, dtype=jnp.float32) + jitter


def draw_lower_block(key, part):
    return coupling_block(jax.random.fold_in(key, 11))


def draw_upper_block(key, part):
    return coupling_block(jax.random.fold_in(key, 23))


def draw_coarse_inverse(key, part):
    diag_key, jitter_key = jax.random.split(jax.random.fold_in(key, 37))
    diagonal = jnp.exp(jax.random.uniform(diag_key, (N_LINE, N_TX, NAGG, CB), jnp.float32, math.log(0.5), math.log(2.0)))
    jitter = 0.3 * jax.random.normal(jitter_key, (N_LINE, N_TX, NAGG, CB, CB), jnp.float32) * CB ** (-0.5)
    return jitter + diagonal[..., None] * jnp.eye(CB, dtype=jnp.float32)


def set_ends(drawn, rng, least, top_value):
    extent = drawn.shape
    index_at = [jax.random.randint(jax.random.fold_in(rng, axis), (), 0, extent[axis]) for axis in range(len(extent))]
    drawn = drawn.at[tuple(index_at)].set(least)
    longest = extent.index(max(extent))
    index_at[longest] = (index_at[longest] + 1) % extent[longest]
    return drawn.at[tuple(index_at)].set(top_value)


def level_of(own_key, dims, pieces, low, largest):
    def one(position, parts):
        draws = jax.random.uniform(jax.random.fold_in(jax.random.fold_in(own_key, 6), position), (parts,), jnp.float32, low / len(pieces), largest / len(pieces))
        return jnp.repeat(jnp.exp(draws), dims[position] // parts).reshape((-1,) + (1,) * (len(dims) - position - 1))

    level = one(*pieces[0])
    for cut in pieces[1:]:
        level = level * one(*cut)
    return level


def noise(key, dims, scale, limit, shards=(), kind=jnp.bfloat16):
    entries = jax.random.normal(key, dims, jnp.float32) * scale
    if len(shards) > 0:
        entries = level_of(key, dims, shards, -0.22, 0.18) * entries
    return jnp.clip(entries, min=-limit, max=limit).astype(kind)


def setup_inputs(seed: int = 0) -> dict:
    key_list = jax.random.split(jax.random.key(seed), 14)
    right_side = noise(key_list[0], (LINES, NX, NY, B), 0.5, 3.0, ((0, 4), (1, 2), (2, 4)), jnp.float32)
    start_field = noise(key_list[1], (LINES, NX, NY, B), 0.5, 3.0, ((0, 4), (1, 2), (2, 4)), jnp.float32)
    line_inverse = draw_line_inverse(jax.random.fold_in(key_list[13], 71), 0)
    lower_scale = jnp.clip(jnp.exp(math.log(1.0) - 0.1625189 * jax.random.uniform(key_list[3], (LINES, NX, NY), jnp.float32) ** level_of(key_list[3], (LINES, NX, NY), ((0, 4), (1, 2), (2, 4)), -0.2, 0.2)), 0.85, 1.0)
    upper_scale = jnp.clip(jnp.exp(math.log(1.0) - 0.1625189 * jax.random.uniform(key_list[4], (LINES, NX, NY), jnp.float32) ** level_of(key_list[4], (LINES, NX, NY), ((0, 4), (1, 2), (2, 4)), -0.2, 0.2)), 0.85, 1.0)
    lower_block = draw_lower_block(jax.random.fold_in(key_list[13], 71), 0)
    upper_block = draw_upper_block(jax.random.fold_in(key_list[13], 71), 0)
    face_blocks = noise(key_list[7], (4, B, B), (11 * B) ** -0.5, 0.15625, (), jnp.float32)
    face_kind = set_ends(jax.random.randint(key_list[8], (4, LINES, NX, NY), 0, 4), jax.random.fold_in(key_list[8], 1), 0, 3).astype(jnp.int32)
    face_scale = jnp.clip(jnp.exp(math.log(1.0) - 1.3862944 * jax.random.uniform(key_list[9], (4, LINES, NX, NY), jnp.float32) ** level_of(key_list[9], (4, LINES, NX, NY), ((1, 4), (2, 2), (3, 4)), -0.2, 0.2)), 0.25, 1.0)
    agglomerate = set_ends(jax.random.randint(key_list[10], (LINES, NX, NY), 0, NAGG), jax.random.fold_in(key_list[10], 1), 0, NAGG - 1).astype(jnp.int32)
    restriction = noise(key_list[11], (CB, B), B ** -0.5, 0.5, (), jnp.float32)
    coarse_inverse = draw_coarse_inverse(jax.random.fold_in(key_list[13], 71), 0)
    return {"right_side": right_side, "start_field": start_field, "line_inverse": line_inverse, "lower_scale": lower_scale, "upper_scale": upper_scale, "lower_block": lower_block, "upper_block": upper_block, "face_blocks": face_blocks, "face_kind": face_kind, "face_scale": face_scale, "agglomerate": agglomerate, "restriction": restriction, "coarse_inverse": coarse_inverse}


highest = lax.Precision.HIGHEST


def couple(field, face_blocks, face_kind, face_scale):
    padded = jnp.pad(field, ((0, 0), (1, 1), (1, 1), (0, 0)))
    beside = (padded[:, :-2, 1:-1], padded[:, 2:, 1:-1], padded[:, 1:-1, :-2], padded[:, 1:-1, 2:])
    total = jnp.zeros_like(field)
    kinds = jnp.arange(4, dtype=jnp.int32)
    for side in range(4):
        images = jnp.einsum('sxyb,kcb->ksxyc', beside[side], face_blocks, precision=highest)
        chosen = (face_kind[side][None] == kinds[:, None, None, None]).astype(jnp.float32)
        picked = jnp.sum(chosen[..., None] * images, axis=0)
        total = total + face_scale[side][..., None] * picked
    return total


def forward(line_inverse, lower_scale, lower_block, drive, start):
    def step(carry, items):
        inverse, scale, source = items
        inner = source - scale[..., None] * jnp.einsum('cb,xyb->xyc', lower_block, carry, precision=highest)
        value = jnp.einsum('xycb,xyb->xyc', inverse.astype(jnp.float32), inner, precision=highest)
        return value, value
    final, values = lax.scan(step, start, (line_inverse, lower_scale, drive))
    return values


def backward(line_inverse, upper_scale, upper_block, ahead, start):
    def step(carry, items):
        inverse, scale, source = items
        inner = scale[..., None] * jnp.einsum('cb,xyb->xyc', upper_block, carry, precision=highest)
        value = source - jnp.einsum('xycb,xyb->xyc', inverse.astype(jnp.float32), inner, precision=highest)
        return value, value
    final, values = lax.scan(step, start, (line_inverse, upper_scale, ahead), reverse=True)
    return values


def reference(right_side, start_field, line_inverse, lower_scale, upper_scale, lower_block, upper_block, face_blocks, face_kind, face_scale, agglomerate, restriction, coarse_inverse):
    empty = jnp.zeros(right_side.shape[1:], jnp.float32)
    field = start_field
    previous = start_field
    for sweep in range(SWEEPS):
        previous = field
        drive = right_side - couple(previous, face_blocks, face_kind, face_scale)
        ahead = forward(line_inverse, lower_scale, lower_block, drive, empty)
        field = backward(line_inverse, upper_scale, upper_block, ahead, empty)
    residual = couple(previous - field, face_blocks, face_kind, face_scale)
    blocks = residual.reshape(N_LINE, SEG, N_TX, LX, NY, B).transpose(0, 2, 1, 3, 4, 5).reshape(N_LINE, N_TX, SEG * LX * NY, B)
    owners = agglomerate.reshape(N_LINE, SEG, N_TX, LX, NY).transpose(0, 2, 1, 3, 4).reshape(N_LINE, N_TX, SEG * LX * NY)
    chosen = (owners[..., None] == jnp.arange(NAGG, dtype=jnp.int32)).astype(jnp.float32)
    projected = jnp.einsum('cb,lteb->ltec', restriction, blocks, precision=highest)
    coarse_sums = jnp.einsum('ltea,ltec->ltac', chosen, projected, precision=highest)
    update = jnp.einsum('ltacd,ltad->ltac', coarse_inverse, coarse_sums, precision=highest)
    spread = jnp.einsum('ltea,ltac->ltec', chosen, update, precision=highest)
    fine = jnp.einsum('cb,ltec->lteb', restriction, spread, precision=highest)
    correction = fine.reshape(N_LINE, N_TX, SEG, LX, NY, B).transpose(0, 2, 1, 3, 4, 5).reshape(right_side.shape)
    return field + correction, residual
```

```python
import functools

import jax
import jax.numpy as jnp
from jax import lax
from jax.experimental import pallas as pl
from jax.experimental.pallas import tpu as pltpu
from jax.sharding import PartitionSpec as P

SWEEPS = 2
MESH = pl.DeviceIdType.MESH
F32 = jnp.float32
BF16 = jnp.bfloat16


def split(x):
    hi = x.astype(BF16)
    lo = (x - hi.astype(F32)).astype(BF16)
    return hi, lo


def wide(x):
    return jnp.concatenate(split(x), axis=1)


def tall(x):
    return jnp.concatenate(split(x), axis=0)


def dot(a, b):
    return jnp.dot(a, b, preferred_element_type=F32)


def quadrants(r):
    m, n = r.shape[0] // 2, r.shape[1] // 2
    return (r[:m, :n] + r[m:, :n]) + (r[:m, n:] + r[m:, n:])


def kernel(
    seg, lx, ly, width, owned, cb, n_line, n_tx, n_ty,
    rhs_ref, start_ref, inv_hbm, ls_ref, us_ref, low_ref, upp_ref, fb_ref, kind_ref, scale_ref, agg_ref,
    rm_ref, ci_ref,
    corr_ref, res_ref,
    inv_ref, invt_ref, q_ref, p_ref, ff_ref, f_ref, g_ref, h_ref,
    mask_ref, lu_ref, wf_ref, rmt_ref, rm4_ref, coef_ref, nb0_ref, nb1_ref, nb2_ref, nb3_ref,
    field_ref, diff_ref, base_ref,
    sx_ref, sy_ref, hx_ref, hy_ref, us_buf, ur_buf, ds_buf, dr_buf,
    abuf, cbuf, pbuf, oht_ref, ct_ref,
    inv_sem, hs_sem, hr_sem, uss_sem, usr_sem, dss_sem, dsr_sem, as_sem, ar_sem, cs_sem, cr_sem, ps_sem, pr_sem,
):
    lines = lx * ly
    rows = seg * lines
    line, tx, ty = lax.axis_index("line"), lax.axis_index("tx"), lax.axis_index("ty")
    has = (tx > 0, tx < n_tx - 1, ty > 0, ty < n_ty - 1)

    inv_copy = pltpu.make_async_copy(inv_hbm, inv_ref, inv_sem)
    inv_copy.start()

    def to_peer(o):
        return {"ty": lax.rem(ty + o, n_ty)}

    barrier = pltpu.get_barrier_semaphore()
    near = (
        (has[0], {"tx": tx - 1}), (has[1], {"tx": tx + 1}),
        (line > 0, {"line": line - 1}), (line < n_line - 1, {"line": line + 1}),
    )
    for there, device in near:
        @pl.when(there)
        def _(device=device):
            pl.semaphore_signal(barrier, inc=1, device_id=device, device_id_type=MESH)
    for o in range(1, n_ty):
        pl.semaphore_signal(barrier, inc=1, device_id=to_peer(o), device_id_type=MESH)

    def pack(source, turn):
        for i in range(seg):
            sx_ref[turn, 0, i * ly:(i + 1) * ly] = source[i * lines:i * lines + ly]
            sx_ref[turn, 1, i * ly:(i + 1) * ly] = source[(i + 1) * lines - ly:(i + 1) * lines]
        sy_ref[turn, 0] = source[pl.ds(0, seg * lx, stride=ly), :]
        sy_ref[turn, 1] = source[pl.ds(ly - 1, seg * lx, stride=ly), :]

    def remote(src, dst, ssem, rsem, device):
        return pltpu.make_async_remote_copy(
            src_ref=src, dst_ref=dst, send_sem=ssem, recv_sem=rsem, device_id=device, device_id_type=MESH
        )

    def halo(turn, side):
        send, land = (sx_ref, hx_ref) if side < 2 else (sy_ref, hy_ref)
        step = 1 if side % 2 else -1
        device = {"tx": tx + step} if side < 2 else {"ty": ty + step}
        other = side + 1 - 2 * (side % 2)
        return remote(
            send.at[turn, side % 2], land.at[turn, other % 2], hs_sem.at[turn, side], hr_sem.at[turn, other], device
        )

    def arriving(turn, side):
        send, land = (sx_ref, hx_ref) if side < 2 else (sy_ref, hy_ref)
        device = {"tx": tx} if side < 2 else {"ty": ty}
        return remote(
            send.at[turn, side % 2], land.at[turn, side % 2], hs_sem.at[turn, side], hr_sem.at[turn, side], device
        )

    def send_halos(turn):
        for side in (2, 3, 0, 1):
            @pl.when(has[side])
            def _(side=side):
                halo(turn, side).start()

    def wait_halos(turn):
        for side in (0, 1, 2, 3):
            @pl.when(has[side])
            def _(side=side):
                arriving(turn, side).wait_recv()

    field_ref[...] = start_ref[...]
    pack(field_ref, 0)
    peers = n_ty - 1
    for there, _device in near:
        peers = peers + jnp.where(there, 1, 0)
    pl.semaphore_wait(barrier, peers)
    send_halos(0)

    for side in range(4):
        @pl.when(jnp.logical_not(has[side]))
        def _(side=side):
            land = hx_ref if side < 2 else hy_ref
            for turn in range(SWEEPS + 1):
                land[turn, side % 2] = jnp.zeros(land.shape[2:], F32)

    @pl.loop(0, rows)
    def _(e):
        i = lax.div(e, lines)
        l = lax.rem(e, lines)
        j = lax.div(l, ly)
        k = lax.rem(l, ly)
        for side in range(4):
            value = scale_ref[side, i, j, k]
            kind = kind_ref[side, i, j, k]
            for w in range(4):
                coef_ref[side * 4 + w, pl.ds(e, 1), :] = jnp.full(
                    (1, width), jnp.where(kind == w, value, 0.0), F32
                )
        abuf[0, pl.ds(e, 1), :] = jnp.full((1, width), agg_ref[i, j, k].astype(F32), F32)

    cbuf[0] = ci_ref[...]

    def agg_copy(o):
        return remote(abuf.at[0], abuf.at[o], as_sem.at[o], ar_sem.at[o], to_peer(o))

    def ci_copy(o):
        return remote(cbuf.at[0], cbuf.at[o], cs_sem.at[o], cr_sem.at[o], to_peer(o))

    def proj_copy(o):
        return remote(pbuf.at[0], pbuf.at[o], ps_sem.at[o], pr_sem.at[o], to_peer(o))

    for o in range(1, n_ty):
        agg_copy(o).start()
        ci_copy(o).start()

    row = lax.broadcasted_iota(jnp.int32, (2 * lines, width), 0)
    for l in range(lines):
        chosen = jnp.logical_or(row == l, row == l + lines)
        mask_ref[:, l * width:(l + 1) * width] = jnp.where(chosen, 1.0, 0.0).astype(BF16)
    eye = (
        lax.broadcasted_iota(jnp.int32, (width, width), 0) == lax.broadcasted_iota(jnp.int32, (width, width), 1)
    )
    lu_ref[0:2 * width] = tall(low_ref[...].T)
    lu_ref[2 * width:4 * width] = tall(upp_ref[...].T)
    lu_ref[4 * width:5 * width] = jnp.where(eye, 1.0, 0.0).astype(BF16)
    for w in range(4):
        wf_ref[w * width:(w + 1) * width] = wide(fb_ref[w].T)
    rep = width // cb
    rm4 = jnp.concatenate([rm_ref[...]] * rep, axis=0)
    rm4_ref[...] = wide(rm4)
    rmt_ref[...] = wide(rm4.T)

    inv_copy.wait()

    for i in range(seg):
        @pl.loop(0, lines, unroll=2)
        def _(l, i=i):
            j = lax.div(l, ly)
            k = lax.rem(l, ly)
            r = lax.dot_general(
                lu_ref[...], inv_ref[i, l], (((1,), (1,)), ((), ())), preferred_element_type=F32
            )
            at = pl.ds(pl.multiple_of(l * width, width), width)
            q_ref[i, at, :] = wide(ls_ref[i, j, k] * (r[0:width] + r[width:2 * width]))
            p_ref[i, at, :] = wide(us_ref[i, j, k] * (r[2 * width:3 * width] + r[3 * width:4 * width]))
            if i == 0:
                ff_ref[0, at, :] = -ls_ref[i, j, k] * (r[0:width] + r[width:2 * width])
            if i == seg - 1:
                h = -us_ref[i, j, k] * (r[2 * width:3 * width] + r[3 * width:4 * width])
                h_ref[i, at, :] = wide(h)
            invt_ref[i, at, :] = r[4 * width:5 * width].astype(BF16)

    def forward_maps():
        for i in range(1, seg):
            @pl.loop(0, lines, unroll=4)
            def _(l, i=i):
                at = pl.ds(pl.multiple_of(l * width, width), width)
                ff_ref[i, at, :] = -quadrants(dot(tall(ff_ref[i - 1, at, :]), q_ref[i, at, :]))

        @pl.loop(0, lines, unroll=2)
        def _(l):
            at = pl.ds(pl.multiple_of(l * width, width), width)
            both = wide(ff_ref[seg - 1, at, :])
            f_ref[at, :] = both
            g_ref[seg - 1, at, :] = both

    def backward_maps():
        for i in range(seg - 2, -1, -1):
            @pl.loop(0, lines, unroll=4)
            def _(l, i=i):
                at = pl.ds(pl.multiple_of(l * width, width), width)
                g = g_ref[i + 1, at, :]
                h = h_ref[i + 1, at, :]
                lhs = jnp.concatenate([g[:, :width], g[:, width:], h[:, :width], h[:, width:]], axis=0)
                r = dot(lhs, p_ref[i, at, :])
                g_ref[i, at, :] = wide(ff_ref[i, at, :] - quadrants(r[:2 * width]))
                h_ref[i, at, :] = wide(-quadrants(r[2 * width:]))

    def spread(x):
        return jnp.concatenate([tall(x)] * lines, axis=1) * mask_ref[...]

    def apply(x, weights):
        return quadrants(dot(spread(x), weights))

    def coupled(v, turn):
        wait_halos(turn)
        nb0_ref[...] = pltpu.roll(v, ly, 0)
        nb1_ref[...] = pltpu.roll(v, rows - ly, 0)
        nb2_ref[...] = pltpu.roll(v, 1, 0)
        nb3_ref[...] = pltpu.roll(v, rows - 1, 0)
        for i in range(seg):
            nb0_ref[i * lines:i * lines + ly] = hx_ref[turn, 0, i * ly:(i + 1) * ly]
            nb1_ref[(i + 1) * lines - ly:(i + 1) * lines] = hx_ref[turn, 1, i * ly:(i + 1) * ly]
        nb2_ref[pl.ds(0, seg * lx, stride=ly), :] = hy_ref[turn, 0]
        nb3_ref[pl.ds(ly - 1, seg * lx, stride=ly), :] = hy_ref[turn, 1]
        beside = (nb0_ref[...], nb1_ref[...], nb2_ref[...], nb3_ref[...])
        left = []
        for w in range(4):
            total = coef_ref[w] * beside[0]
            for side in range(1, 4):
                total = total + coef_ref[side * 4 + w] * beside[side]
            left.append(tall(total))
        return quadrants(dot(jnp.concatenate(left, axis=1), wf_ref[...]))

    def up_copy(sweep):
        return remote(us_buf.at[sweep], ur_buf.at[sweep], uss_sem.at[sweep], usr_sem.at[sweep], {"line": line + 1})

    def down_copy(sweep):
        return remote(ds_buf.at[sweep], dr_buf.at[sweep], dss_sem.at[sweep], dsr_sem.at[sweep], {"line": line - 1})

    first, last = line == 0, line == n_line - 1
    late = line >= n_line // 2
    for sweep in range(SWEEPS):
        v = field_ref[...]
        drive = rhs_ref[...] - coupled(v, sweep)
        z = []
        for i in range(seg):
            r = dot(spread(drive[i * lines:(i + 1) * lines]), invt_ref[i])
            z.append(r[:lines] + r[lines:])
            if i > 0:
                z[i] = z[i] - apply(z[i - 1], q_ref[i])

        @pl.when(first)
        def _(sweep=sweep, z=z):
            us_buf[sweep] = z[seg - 1]
            ur_buf[sweep] = jnp.zeros((lines, width), F32)
            if n_line > 1:
                up_copy(sweep).start()

        if sweep == 0:
            forward_maps()
            pl.when(late)(backward_maps)
        w = [None] * seg
        w[seg - 1] = z[seg - 1]
        for i in range(seg - 2, -1, -1):
            w[i] = z[i] - apply(w[i + 1], p_ref[i])
        for i in range(seg):
            base_ref[i] = w[i]

        @pl.when(jnp.logical_not(first))
        def _(sweep=sweep, z=z):
            up_copy(sweep).wait_recv()

            @pl.when(jnp.logical_not(last))
            def _():
                us_buf[sweep] = z[seg - 1] + apply(ur_buf[sweep], f_ref[...])
                up_copy(sweep).start()

        if sweep == 0:
            pl.when(jnp.logical_not(late))(backward_maps)
        incoming = spread(ur_buf[sweep])
        base = base_ref[0] + quadrants(dot(incoming, g_ref[0]))
        base_ref[0] = base

        @pl.when(last)
        def _(sweep=sweep, base=base):
            ds_buf[sweep] = base
            dr_buf[sweep] = jnp.zeros((lines, width), F32)
            if n_line > 1:
                down_copy(sweep).start()

        for i in range(1, seg):
            base_ref[i] = base_ref[i] + quadrants(dot(incoming, g_ref[i]))

        @pl.when(jnp.logical_not(last))
        def _(sweep=sweep):
            down_copy(sweep).wait_recv()

        behind = spread(dr_buf[sweep])
        x = base_ref[0] + quadrants(dot(behind, h_ref[0]))

        @pl.when(jnp.logical_not(jnp.logical_or(first, last)))
        def _(sweep=sweep, x=x):
            ds_buf[sweep] = x
            down_copy(sweep).start()

        field_ref[0:lines] = x
        for i in range(1, seg):
            field_ref[i * lines:(i + 1) * lines] = base_ref[i] + quadrants(dot(behind, h_ref[i]))
        if sweep < SWEEPS - 1:
            pack(field_ref, sweep + 1)
            send_halos(sweep + 1)
        else:
            diff_ref[...] = v - field_ref[...]
            pack(diff_ref, sweep + 1)
            send_halos(sweep + 1)

    aggs = oht_ref.shape[0]
    for o in range(1, n_ty):
        agg_copy(o).wait_recv()
        ci_copy(o).wait_recv()
    for o in range(n_ty):
        ids = abuf[o].T
        for b in range(aggs // width):
            index = lax.broadcasted_iota(jnp.int32, (width, rows), 0) + b * width
            oht_ref[b * width:(b + 1) * width, o * rows:(o + 1) * rows] = jnp.where(
                ids == index.astype(F32), 1.0, 0.0
            ).astype(BF16)
        ct_ref[:, 2 * o * width:2 * (o + 1) * width] = wide(cbuf[o].T)

    residual = coupled(diff_ref[...], SWEEPS)
    res_ref[...] = residual
    pbuf[0] = quadrants(dot(tall(residual), rmt_ref[...]))
    for o in range(1, n_ty):
        proj_copy(o).start()

    a_row = lax.broadcasted_iota(jnp.int32, (aggs, width), 0)
    group = lax.div(lax.broadcasted_iota(jnp.int32, (aggs, width), 1), cb)
    within = lax.rem(a_row, rep)
    own_ids = abuf[0]
    chosen = []
    for b in range(aggs // width):
        index = lax.broadcasted_iota(jnp.int32, (rows, width), 1) + b * width
        chosen.append(jnp.where(own_ids == index.astype(F32), 1.0, 0.0).astype(BF16))
    for o in range(1, n_ty):
        proj_copy(o).wait_recv()
    gathered = wide(pbuf[...].reshape(n_ty * rows, width))
    sums = dot(oht_ref[...], gathered)
    sums = sums[:, :width] + sums[:, width:]
    sums = jnp.where(group == within, sums, 0.0)
    images = dot(tall(sums), ct_ref[...])
    update = jnp.zeros((aggs, width), F32)
    for o in range(n_ty):
        part = quadrants(images[:, 2 * o * width:2 * (o + 1) * width])
        owner = lax.rem(ty + (n_ty - o), n_ty)
        update = update + jnp.where(owner * owned + group * rep + within == a_row, part, 0.0)
    fine = quadrants(dot(tall(update), rm4_ref[...]))
    r = dot(jnp.concatenate(chosen, axis=1), wide(fine))
    corr_ref[...] = field_ref[...] + (r[:, :width] + r[:, width:])

    for turn in range(SWEEPS + 1):
        for side in range(4):
            @pl.when(has[side])
            def _(turn=turn, side=side):
                halo(turn, side).wait_send()
    for sweep in range(SWEEPS):
        @pl.when(jnp.logical_not(last))
        def _(sweep=sweep):
            up_copy(sweep).wait_send()

        @pl.when(jnp.logical_not(first))
        def _(sweep=sweep):
            down_copy(sweep).wait_send()
    for o in range(1, n_ty):
        agg_copy(o).wait_send()
        ci_copy(o).wait_send()
        proj_copy(o).wait_send()


def body(
    right_side, start_field, line_inverse, lower_scale, upper_scale, lower_block, upper_block, face_blocks,
    face_kind, face_scale, agglomerate, restriction, coarse_inverse,
):
    seg, lx, ly, width = right_side.shape
    owned, cb = coarse_inverse.shape[2:4]
    lines = lx * ly
    rows = seg * lines
    n_line, n_tx, n_ty = (lax.axis_size(axis) for axis in ("line", "tx", "ty"))
    rep = width // cb
    groups = owned // rep
    assert rep * cb == width and groups == rep and groups * rep == owned
    aggs = -(-owned * n_ty // width) * width
    blocks = coarse_inverse.reshape(groups, rep, cb, cb).transpose(0, 2, 1, 3).reshape(width, width)
    tall_k = lines * width
    vmem, smem = pl.BlockSpec(memory_space=pltpu.VMEM), pl.BlockSpec(memory_space=pltpu.SMEM)
    dma = pltpu.SemaphoreType.DMA
    turns = SWEEPS + 1
    scratch = [
        pltpu.VMEM((seg, lines, width, width), BF16),
        pltpu.VMEM((seg, tall_k, width), BF16),
        pltpu.VMEM((seg, tall_k, 2 * width), BF16),
        pltpu.VMEM((seg, tall_k, 2 * width), BF16),
        pltpu.VMEM((seg, tall_k, width), F32),
        pltpu.VMEM((tall_k, 2 * width), BF16),
        pltpu.VMEM((seg, tall_k, 2 * width), BF16),
        pltpu.VMEM((seg, tall_k, 2 * width), BF16),
        pltpu.VMEM((2 * lines, tall_k), BF16),
        pltpu.VMEM((5 * width, width), BF16),
        pltpu.VMEM((4 * width, 2 * width), BF16),
        pltpu.VMEM((width, 2 * width), BF16),
        pltpu.VMEM((width, 2 * width), BF16),
        pltpu.VMEM((16, rows, width), F32),
        pltpu.VMEM((rows, width), F32),
        pltpu.VMEM((rows, width), F32),
        pltpu.VMEM((rows, width), F32),
        pltpu.VMEM((rows, width), F32),
        pltpu.VMEM((rows, width), F32),
        pltpu.VMEM((rows, width), F32),
        pltpu.VMEM((seg, lines, width), F32),
        pltpu.VMEM((turns, 2, seg * ly, width), F32),
        pltpu.VMEM((turns, 2, seg * lx, width), F32),
        pltpu.VMEM((turns, 2, seg * ly, width), F32),
        pltpu.VMEM((turns, 2, seg * lx, width), F32),
        pltpu.VMEM((SWEEPS, lines, width), F32),
        pltpu.VMEM((SWEEPS, lines, width), F32),
        pltpu.VMEM((SWEEPS, lines, width), F32),
        pltpu.VMEM((SWEEPS, lines, width), F32),
        pltpu.VMEM((n_ty, rows, width), F32),
        pltpu.VMEM((n_ty, width, width), F32),
        pltpu.VMEM((n_ty, rows, width), F32),
        pltpu.VMEM((aggs, n_ty * rows), BF16),
        pltpu.VMEM((width, 2 * n_ty * width), BF16),
        dma, dma((turns, 4)), dma((turns, 4)),
        dma((SWEEPS,)), dma((SWEEPS,)), dma((SWEEPS,)), dma((SWEEPS,)),
        dma((n_ty,)), dma((n_ty,)), dma((n_ty,)), dma((n_ty,)), dma((n_ty,)), dma((n_ty,)),
    ]
    flat = jax.ShapeDtypeStruct((rows, width), F32)
    corrected, residual = pl.pallas_call(
        functools.partial(kernel, seg, lx, ly, width, owned, cb, n_line, n_tx, n_ty),
        out_shape=(flat, flat),
        in_specs=[
            vmem, vmem, pl.BlockSpec(memory_space=pl.ANY), smem, smem, vmem, vmem, vmem, smem, smem, smem, vmem, vmem,
        ],
        out_specs=(vmem, vmem),
        scratch_shapes=scratch,
        compiler_params=pltpu.CompilerParams(
            collective_id=0, has_side_effects=True, vmem_limit_bytes=60 * 2**20
        ),
    )(
        right_side.reshape(rows, width), start_field.reshape(rows, width),
        line_inverse.reshape(seg, lines, width, width), lower_scale, upper_scale, lower_block, upper_block,
        face_blocks, face_kind, face_scale, agglomerate, restriction, blocks,
    )
    return corrected.reshape(right_side.shape), residual.reshape(right_side.shape)


def solution(mesh):
    in_specs = (
        P("line", "tx", "ty", None),
        P("line", "tx", "ty", None),
        P("line", "tx", "ty", None, None),
        P("line", "tx", "ty"),
        P("line", "tx", "ty"),
        P(),
        P(),
        P(),
        P(None, "line", "tx", "ty"),
        P(None, "line", "tx", "ty"),
        P("line", "tx", "ty"),
        P(),
        P("line", "tx", "ty", None, None),
    )
    out_specs = (P("line", "tx", "ty", None), P("line", "tx", "ty", None))
    return jax.shard_map(body, mesh=mesh, in_specs=in_specs, out_specs=out_specs, check_vma=False)
```

```python
import functools

import jax
import jax.numpy as jnp
from jax import lax
from jax.experimental import pallas as pl
from jax.experimental.pallas import tpu as pltpu
from jax.sharding import PartitionSpec as P

SWEEPS = 2
MESH = pl.DeviceIdType.MESH
F32 = jnp.float32
BF16 = jnp.bfloat16


def split(x):
    hi = x.astype(BF16)
    lo = (x - hi.astype(F32)).astype(BF16)
    return hi, lo


def wide(x):
    return jnp.concatenate(split(x), axis=1)


def tall(x):
    return jnp.concatenate(split(x), axis=0)


def dot(a, b):
    return jnp.dot(a, b, preferred_element_type=F32)


def quadrants(r):
    m, n = r.shape[0] // 2, r.shape[1] // 2
    return (r[:m, :n] + r[m:, :n]) + (r[:m, n:] + r[m:, n:])


def kernel(
    seg, lx, ly, width, owned, cb, n_line, n_tx, n_ty,
    rhs_ref, start_ref, inv_hbm, ls_ref, us_ref, low_ref, upp_ref, fb_ref, kind_ref, scale_ref, agg_ref,
    rm_ref, ci_ref,
    corr_ref, res_ref,
    inv_ref, invt_ref, q_ref, p_ref, ff_ref, f_ref, g_ref, h_ref,
    mask_ref, lu_ref, wf_ref, rmt_ref, rm4_ref, coef_ref, nb0_ref, nb1_ref, nb2_ref, nb3_ref,
    field_ref, diff_ref, base_ref,
    sx_ref, sy_ref, hx_ref, hy_ref, us_buf, ur_buf, ds_buf, dr_buf,
    abuf, cbuf, pbuf, oht_ref, ct_ref,
    inv_sem, hs_sem, hr_sem, uss_sem, usr_sem, dss_sem, dsr_sem, as_sem, ar_sem, cs_sem, cr_sem, ps_sem, pr_sem,
):
    lines = lx * ly
    rows = seg * lines
    line, tx, ty = lax.axis_index("line"), lax.axis_index("tx"), lax.axis_index("ty")
    has = (tx > 0, tx < n_tx - 1, ty > 0, ty < n_ty - 1)

    inv_copy = pltpu.make_async_copy(inv_hbm, inv_ref, inv_sem)
    inv_copy.start()

    def to_peer(o):
        return {"ty": lax.rem(ty + o, n_ty)}

    barrier = pltpu.get_barrier_semaphore()
    near = (
        (has[0], {"tx": tx - 1}), (has[1], {"tx": tx + 1}),
        (line > 0, {"line": line - 1}), (line < n_line - 1, {"line": line + 1}),
    )
    for there, device in near:
        @pl.when(there)
        def _(device=device):
            pl.semaphore_signal(barrier, inc=1, device_id=device, device_id_type=MESH)
    for o in range(1, n_ty):
        pl.semaphore_signal(barrier, inc=1, device_id=to_peer(o), device_id_type=MESH)

    def pack(source, turn):
        for i in range(seg):
            sx_ref[turn, 0, i * ly:(i + 1) * ly] = source[i * lines:i * lines + ly]
            sx_ref[turn, 1, i * ly:(i + 1) * ly] = source[(i + 1) * lines - ly:(i + 1) * lines]
        sy_ref[turn, 0] = source[pl.ds(0, seg * lx, stride=ly), :]
        sy_ref[turn, 1] = source[pl.ds(ly - 1, seg * lx, stride=ly), :]

    def remote(src, dst, ssem, rsem, device):
        return pltpu.make_async_remote_copy(
            src_ref=src, dst_ref=dst, send_sem=ssem, recv_sem=rsem, device_id=device, device_id_type=MESH
        )

    def halo(turn, side):
        send, land = (sx_ref, hx_ref) if side < 2 else (sy_ref, hy_ref)
        step = 1 if side % 2 else -1
        device = {"tx": tx + step} if side < 2 else {"ty": ty + step}
        other = side + 1 - 2 * (side % 2)
        return remote(
            send.at[turn, side % 2], land.at[turn, other % 2], hs_sem.at[turn, side], hr_sem.at[turn, other], device
        )

    def arriving(turn, side):
        send, land = (sx_ref, hx_ref) if side < 2 else (sy_ref, hy_ref)
        device = {"tx": tx} if side < 2 else {"ty": ty}
        return remote(
            send.at[turn, side % 2], land.at[turn, side % 2], hs_sem.at[turn, side], hr_sem.at[turn, side], device
        )

    def send_halos(turn):
        for side in (2, 3, 0, 1):
            @pl.when(has[side])
            def _(side=side):
                halo(turn, side).start()

    def wait_halos(turn):
        for side in (0, 1, 2, 3):
            @pl.when(has[side])
            def _(side=side):
                arriving(turn, side).wait_recv()

    field_ref[...] = start_ref[...]
    pack(field_ref, 0)
    peers = n_ty - 1
    for there, _device in near:
        peers = peers + jnp.where(there, 1, 0)
    pl.semaphore_wait(barrier, peers)
    send_halos(0)

    for side in range(4):
        @pl.when(jnp.logical_not(has[side]))
        def _(side=side):
            land = hx_ref if side < 2 else hy_ref
            for turn in range(SWEEPS + 1):
                land[turn, side % 2] = jnp.zeros(land.shape[2:], F32)

    @pl.loop(0, rows, unroll=4)
    def _(e):
        i = lax.div(e, lines)
        l = lax.rem(e, lines)
        j = lax.div(l, ly)
        k = lax.rem(l, ly)
        for side in range(4):
            value = scale_ref[side, i, j, k]
            kind = kind_ref[side, i, j, k]
            for w in range(4):
                coef_ref[side * 4 + w, pl.ds(e, 1), :] = jnp.full(
                    (1, width), jnp.where(kind == w, value, 0.0), F32
                )
        abuf[0, pl.ds(e, 1), :] = jnp.full((1, width), agg_ref[i, j, k].astype(F32), F32)

    rep = width // cb
    placed = jnp.zeros((width, width), F32)
    for a in range(rep):
        stacked = jnp.concatenate([ci_ref[t * rep + a] for t in range(rep)], axis=0)
        lane = lax.broadcasted_iota(jnp.int32, (cb, width), 1)
        place = lane == lax.broadcasted_iota(jnp.int32, (cb, width), 0) + a * cb
        place = jnp.where(place, 1.0, 0.0).astype(BF16)
        for half in split(stacked):
            placed = placed + dot(half, place)
    cbuf[0] = placed

    def agg_copy(o):
        return remote(abuf.at[0], abuf.at[o], as_sem.at[o], ar_sem.at[o], to_peer(o))

    def ci_copy(o):
        return remote(cbuf.at[0], cbuf.at[o], cs_sem.at[o], cr_sem.at[o], to_peer(o))

    def proj_copy(o):
        return remote(pbuf.at[0], pbuf.at[o], ps_sem.at[o], pr_sem.at[o], to_peer(o))

    for o in range(1, n_ty):
        agg_copy(o).start()
        ci_copy(o).start()

    row = lax.broadcasted_iota(jnp.int32, (2 * lines, width), 0)
    for l in range(lines):
        chosen = jnp.logical_or(row == l, row == l + lines)
        mask_ref[:, l * width:(l + 1) * width] = jnp.where(chosen, 1.0, 0.0).astype(BF16)
    eye = (
        lax.broadcasted_iota(jnp.int32, (width, width), 0) == lax.broadcasted_iota(jnp.int32, (width, width), 1)
    )
    lu_ref[0:width] = wide(low_ref[...].T)
    lu_ref[width:2 * width, :width] = jnp.where(eye, 1.0, 0.0).astype(BF16)
    lu_ref[width:2 * width, width:] = jnp.zeros((width, width), BF16)
    lu_ref[2 * width:3 * width] = wide(upp_ref[...].T)
    for w in range(4):
        wf_ref[w * width:(w + 1) * width] = wide(fb_ref[w].T)
    rm4 = jnp.concatenate([rm_ref[...]] * rep, axis=0)
    rm4_ref[...] = wide(rm4)
    rmt_ref[...] = wide(rm4.T)

    inv_copy.wait()

    def at(l):
        return pl.ds(pl.multiple_of(l * width, width), width)

    def folded(i, l, left):
        pair = jnp.concatenate([inv_ref[i, l], inv_ref[i, l + 1]], axis=0)
        pair = jnp.concatenate([pair, pair], axis=1)
        return lax.dot_general(left, pair, (((1,), (1,)), ((), ())), preferred_element_type=F32)

    def halves(r):
        return r[:, :width] + r[:, width:]

    def stacked_twice(w):
        return jnp.concatenate([w, w], axis=0)

    for i in range(seg):
        @pl.loop(0, lines // 2, unroll=2)
        def _(pair, i=i):
            r = folded(i, pair * 2, lu_ref[0:2 * width])
            for m in range(2):
                l = pair * 2 + m
                scale = ls_ref[i, lax.div(l, ly), lax.rem(l, ly)]
                q = scale * r[:width, m * width:(m + 1) * width]
                q_ref[i, at(l), :] = wide(q)
                if i == 0:
                    ff_ref[0, at(l), :] = -q
                invt_ref[i, at(l), :] = r[width:, m * width:(m + 1) * width].astype(BF16)

    def upper_maps():
        for i in range(seg):
            @pl.loop(0, lines // 2, unroll=2)
            def _(pair, i=i):
                r = folded(i, pair * 2, lu_ref[2 * width:3 * width])
                for m in range(2):
                    l = pair * 2 + m
                    scale = us_ref[i, lax.div(l, ly), lax.rem(l, ly)]
                    p = scale * r[:, m * width:(m + 1) * width]
                    p_ref[i, at(l), :] = wide(p)
                    if i == seg - 1:
                        h_ref[i, at(l), :] = wide(-p)

    def forward_maps():
        for i in range(1, seg):
            @pl.loop(0, lines, unroll=4)
            def _(l, i=i):
                f = -halves(dot(wide(ff_ref[i - 1, at(l), :]), stacked_twice(q_ref[i, at(l), :])))
                ff_ref[i, at(l), :] = f
                if i == seg - 1:
                    both = wide(f)
                    f_ref[at(l), :] = both
                    g_ref[i, at(l), :] = both

    def backward_maps():
        for i in range(seg - 2, -1, -1):
            @pl.loop(0, lines, unroll=4)
            def _(l, i=i):
                left = jnp.concatenate([g_ref[i + 1, at(l), :], h_ref[i + 1, at(l), :]], axis=0)
                r = halves(dot(left, stacked_twice(p_ref[i, at(l), :])))
                g_ref[i, at(l), :] = wide(ff_ref[i, at(l), :] - r[:width])
                h_ref[i, at(l), :] = wide(-r[width:])

    def spread(x):
        return jnp.concatenate([tall(x)] * lines, axis=1) * mask_ref[...]

    def apply(x, weights):
        return quadrants(dot(spread(x), weights))

    def coupled(v, turn):
        wait_halos(turn)
        nb0_ref[...] = pltpu.roll(v, ly, 0)
        nb1_ref[...] = pltpu.roll(v, rows - ly, 0)
        nb2_ref[...] = pltpu.roll(v, 1, 0)
        nb3_ref[...] = pltpu.roll(v, rows - 1, 0)
        for i in range(seg):
            nb0_ref[i * lines:i * lines + ly] = hx_ref[turn, 0, i * ly:(i + 1) * ly]
            nb1_ref[(i + 1) * lines - ly:(i + 1) * lines] = hx_ref[turn, 1, i * ly:(i + 1) * ly]
        nb2_ref[pl.ds(0, seg * lx, stride=ly), :] = hy_ref[turn, 0]
        nb3_ref[pl.ds(ly - 1, seg * lx, stride=ly), :] = hy_ref[turn, 1]
        beside = (nb0_ref[...], nb1_ref[...], nb2_ref[...], nb3_ref[...])
        left = []
        for w in range(4):
            total = coef_ref[w] * beside[0]
            for side in range(1, 4):
                total = total + coef_ref[side * 4 + w] * beside[side]
            left.append(tall(total))
        return quadrants(dot(jnp.concatenate(left, axis=1), wf_ref[...]))

    def up_copy(sweep):
        return remote(us_buf.at[sweep], ur_buf.at[sweep], uss_sem.at[sweep], usr_sem.at[sweep], {"line": line + 1})

    def down_copy(sweep):
        return remote(ds_buf.at[sweep], dr_buf.at[sweep], dss_sem.at[sweep], dsr_sem.at[sweep], {"line": line - 1})

    first, last = line == 0, line == n_line - 1
    late = line >= n_line // 2
    def early(sweep):
        drive = rhs_ref[...] - coupled(field_ref[...], sweep)
        for i in range(seg):
            r = dot(spread(drive[i * lines:(i + 1) * lines]), invt_ref[i])
            base_ref[i] = r[:lines] + r[lines:]

        @pl.when(late)
        def _():
            upper_maps()
            forward_maps()

        pl.when(last)(backward_maps)

        @pl.when(first)
        def _():
            ur_buf[sweep] = jnp.zeros((lines, width), F32)

        @pl.when(jnp.logical_not(first))
        def _():
            up_copy(sweep).wait_recv()

        y = ur_buf[sweep]
        for i in range(seg):
            y = base_ref[i] - apply(y, q_ref[i])
            base_ref[i] = y

        @pl.when(jnp.logical_not(last))
        def _():
            us_buf[sweep] = y
            up_copy(sweep).start()

        @pl.when(jnp.logical_not(late))
        def _():
            upper_maps()
            forward_maps()

        pl.when(jnp.logical_not(last))(backward_maps)

        @pl.when(last)
        def _():
            dr_buf[sweep] = jnp.zeros((lines, width), F32)

        @pl.when(jnp.logical_not(last))
        def _():
            down_copy(sweep).wait_recv()

        x = dr_buf[sweep]
        for i in range(seg - 1, -1, -1):
            x = base_ref[i] - apply(x, p_ref[i])
            field_ref[i * lines:(i + 1) * lines] = x

        @pl.when(jnp.logical_not(first))
        def _():
            ds_buf[sweep] = x
            down_copy(sweep).start()

    def mapped(sweep):
        drive = rhs_ref[...] - coupled(field_ref[...], sweep)
        z = []
        for i in range(seg):
            r = dot(spread(drive[i * lines:(i + 1) * lines]), invt_ref[i])
            z.append(r[:lines] + r[lines:])
            if i > 0:
                z[i] = z[i] - apply(z[i - 1], q_ref[i])

        @pl.when(first)
        def _():
            us_buf[sweep] = z[seg - 1]
            ur_buf[sweep] = jnp.zeros((lines, width), F32)
            if n_line > 1:
                up_copy(sweep).start()

        w = [None] * seg
        w[seg - 1] = z[seg - 1]
        for i in range(seg - 2, -1, -1):
            w[i] = z[i] - apply(w[i + 1], p_ref[i])
        for i in range(seg):
            base_ref[i] = w[i]

        @pl.when(jnp.logical_not(first))
        def _():
            up_copy(sweep).wait_recv()

            @pl.when(jnp.logical_not(last))
            def _():
                us_buf[sweep] = z[seg - 1] + apply(ur_buf[sweep], f_ref[...])
                up_copy(sweep).start()

        incoming = spread(ur_buf[sweep])
        base = base_ref[0] + quadrants(dot(incoming, g_ref[0]))
        base_ref[0] = base

        @pl.when(last)
        def _():
            ds_buf[sweep] = base
            dr_buf[sweep] = jnp.zeros((lines, width), F32)
            if n_line > 1:
                down_copy(sweep).start()

        for i in range(1, seg):
            base_ref[i] = base_ref[i] + quadrants(dot(incoming, g_ref[i]))

        @pl.when(jnp.logical_not(last))
        def _():
            down_copy(sweep).wait_recv()

        behind = spread(dr_buf[sweep])
        x = base_ref[0] + quadrants(dot(behind, h_ref[0]))

        @pl.when(jnp.logical_not(jnp.logical_or(first, last)))
        def _():
            ds_buf[sweep] = x
            down_copy(sweep).start()

        field_ref[0:lines] = x
        for i in range(1, seg):
            field_ref[i * lines:(i + 1) * lines] = base_ref[i] + quadrants(dot(behind, h_ref[i]))

    for sweep in range(SWEEPS):
        v = field_ref[...]
        (early if sweep == 0 else mapped)(sweep)
        if sweep < SWEEPS - 1:
            pack(field_ref, sweep + 1)
            send_halos(sweep + 1)
        else:
            diff_ref[...] = v - field_ref[...]
            pack(diff_ref, sweep + 1)
            send_halos(sweep + 1)

    aggs = oht_ref.shape[0]
    for o in range(1, n_ty):
        agg_copy(o).wait_recv()
        ci_copy(o).wait_recv()
    for o in range(n_ty):
        ids = abuf[o].T
        for b in range(aggs // width):
            index = lax.broadcasted_iota(jnp.int32, (width, rows), 0) + b * width
            oht_ref[b * width:(b + 1) * width, o * rows:(o + 1) * rows] = jnp.where(
                ids == index.astype(F32), 1.0, 0.0
            ).astype(BF16)
        ct_ref[:, 2 * o * width:2 * (o + 1) * width] = wide(cbuf[o].T)

    residual = coupled(diff_ref[...], SWEEPS)
    res_ref[...] = residual
    pbuf[0] = quadrants(dot(tall(residual), rmt_ref[...]))
    for o in range(1, n_ty):
        proj_copy(o).start()

    a_row = lax.broadcasted_iota(jnp.int32, (aggs, width), 0)
    group = lax.div(lax.broadcasted_iota(jnp.int32, (aggs, width), 1), cb)
    within = lax.rem(a_row, rep)
    own_ids = abuf[0]
    chosen = []
    for b in range(aggs // width):
        index = lax.broadcasted_iota(jnp.int32, (rows, width), 1) + b * width
        chosen.append(jnp.where(own_ids == index.astype(F32), 1.0, 0.0).astype(BF16))
    for o in range(1, n_ty):
        proj_copy(o).wait_recv()
    gathered = wide(pbuf[...].reshape(n_ty * rows, width))
    sums = dot(oht_ref[...], gathered)
    sums = sums[:, :width] + sums[:, width:]
    sums = jnp.where(group == within, sums, 0.0)
    images = dot(tall(sums), ct_ref[...])
    update = jnp.zeros((aggs, width), F32)
    for o in range(n_ty):
        part = quadrants(images[:, 2 * o * width:2 * (o + 1) * width])
        owner = lax.rem(ty + (n_ty - o), n_ty)
        update = update + jnp.where(owner * owned + group * rep + within == a_row, part, 0.0)
    fine = quadrants(dot(tall(update), rm4_ref[...]))
    r = dot(jnp.concatenate(chosen, axis=1), wide(fine))
    corr_ref[...] = field_ref[...] + (r[:, :width] + r[:, width:])

    for turn in range(SWEEPS + 1):
        for side in range(4):
            @pl.when(has[side])
            def _(turn=turn, side=side):
                halo(turn, side).wait_send()
    for sweep in range(SWEEPS):
        @pl.when(jnp.logical_not(last))
        def _(sweep=sweep):
            up_copy(sweep).wait_send()

        @pl.when(jnp.logical_not(first))
        def _(sweep=sweep):
            down_copy(sweep).wait_send()
    for o in range(1, n_ty):
        agg_copy(o).wait_send()
        ci_copy(o).wait_send()
        proj_copy(o).wait_send()


def body(
    right_side, start_field, line_inverse, lower_scale, upper_scale, lower_block, upper_block, face_blocks,
    face_kind, face_scale, agglomerate, restriction, coarse_inverse,
):
    seg, lx, ly, width = right_side.shape
    owned, cb = coarse_inverse.shape[2:4]
    lines = lx * ly
    rows = seg * lines
    n_line, n_tx, n_ty = (lax.axis_size(axis) for axis in ("line", "tx", "ty"))
    rep = width // cb
    groups = owned // rep
    assert rep * cb == width and groups == rep and groups * rep == owned
    aggs = -(-owned * n_ty // width) * width
    tall_k = lines * width
    vmem, smem = pl.BlockSpec(memory_space=pltpu.VMEM), pl.BlockSpec(memory_space=pltpu.SMEM)
    dma = pltpu.SemaphoreType.DMA
    turns = SWEEPS + 1
    scratch = [
        pltpu.VMEM((seg, lines, width, width), BF16),
        pltpu.VMEM((seg, tall_k, width), BF16),
        pltpu.VMEM((seg, tall_k, 2 * width), BF16),
        pltpu.VMEM((seg, tall_k, 2 * width), BF16),
        pltpu.VMEM((seg, tall_k, width), F32),
        pltpu.VMEM((tall_k, 2 * width), BF16),
        pltpu.VMEM((seg, tall_k, 2 * width), BF16),
        pltpu.VMEM((seg, tall_k, 2 * width), BF16),
        pltpu.VMEM((2 * lines, tall_k), BF16),
        pltpu.VMEM((3 * width, 2 * width), BF16),
        pltpu.VMEM((4 * width, 2 * width), BF16),
        pltpu.VMEM((width, 2 * width), BF16),
        pltpu.VMEM((width, 2 * width), BF16),
        pltpu.VMEM((16, rows, width), F32),
        pltpu.VMEM((rows, width), F32),
        pltpu.VMEM((rows, width), F32),
        pltpu.VMEM((rows, width), F32),
        pltpu.VMEM((rows, width), F32),
        pltpu.VMEM((rows, width), F32),
        pltpu.VMEM((rows, width), F32),
        pltpu.VMEM((seg, lines, width), F32),
        pltpu.VMEM((turns, 2, seg * ly, width), F32),
        pltpu.VMEM((turns, 2, seg * lx, width), F32),
        pltpu.VMEM((turns, 2, seg * ly, width), F32),
        pltpu.VMEM((turns, 2, seg * lx, width), F32),
        pltpu.VMEM((SWEEPS, lines, width), F32),
        pltpu.VMEM((SWEEPS, lines, width), F32),
        pltpu.VMEM((SWEEPS, lines, width), F32),
        pltpu.VMEM((SWEEPS, lines, width), F32),
        pltpu.VMEM((n_ty, rows, width), F32),
        pltpu.VMEM((n_ty, width, width), F32),
        pltpu.VMEM((n_ty, rows, width), F32),
        pltpu.VMEM((aggs, n_ty * rows), BF16),
        pltpu.VMEM((width, 2 * n_ty * width), BF16),
        dma, dma((turns, 4)), dma((turns, 4)),
        dma((SWEEPS,)), dma((SWEEPS,)), dma((SWEEPS,)), dma((SWEEPS,)),
        dma((n_ty,)), dma((n_ty,)), dma((n_ty,)), dma((n_ty,)), dma((n_ty,)), dma((n_ty,)),
    ]
    flat = jax.ShapeDtypeStruct((rows, width), F32)
    corrected, residual = pl.pallas_call(
        functools.partial(kernel, seg, lx, ly, width, owned, cb, n_line, n_tx, n_ty),
        out_shape=(flat, flat),
        in_specs=[
            vmem, vmem, pl.BlockSpec(memory_space=pl.ANY), smem, smem, vmem, vmem, vmem, smem, smem, smem, vmem, vmem,
        ],
        out_specs=(vmem, vmem),
        scratch_shapes=scratch,
        compiler_params=pltpu.CompilerParams(
            collective_id=0, has_side_effects=True, vmem_limit_bytes=60 * 2**20
        ),
    )(
        right_side.reshape(rows, width), start_field.reshape(rows, width),
        line_inverse.reshape(seg, lines, width, width), lower_scale, upper_scale, lower_block, upper_block,
        face_blocks, face_kind, face_scale, agglomerate, restriction,
        coarse_inverse.reshape(owned, cb, cb),
    )
    return corrected.reshape(right_side.shape), residual.reshape(right_side.shape)


def solution(mesh):
    in_specs = (
        P("line", "tx", "ty", None),
        P("line", "tx", "ty", None),
        P("line", "tx", "ty", None, None),
        P("line", "tx", "ty"),
        P("line", "tx", "ty"),
        P(),
        P(),
        P(),
        P(None, "line", "tx", "ty"),
        P(None, "line", "tx", "ty"),
        P("line", "tx", "ty"),
        P(),
        P("line", "tx", "ty", None, None),
    )
    out_specs = (P("line", "tx", "ty", None), P("line", "tx", "ty", None))
    return jax.shard_map(body, mesh=mesh, in_specs=in_specs, out_specs=out_specs, check_vma=False)
```

```python
import functools

import jax
import jax.numpy as jnp
from jax import lax
from jax.experimental import pallas as pl
from jax.experimental.pallas import tpu as pltpu
from jax.sharding import PartitionSpec as P

SWEEPS = 2
MESH = pl.DeviceIdType.MESH
F32 = jnp.float32
BF16 = jnp.bfloat16


def split(x):
    hi = x.astype(BF16)
    lo = (x - hi.astype(F32)).astype(BF16)
    return hi, lo


def wide(x):
    return jnp.concatenate(split(x), axis=1)


def tall(x):
    return jnp.concatenate(split(x), axis=0)


def dot(a, b):
    return jnp.dot(a, b, preferred_element_type=F32)


def quadrants(r):
    m, n = r.shape[0] // 2, r.shape[1] // 2
    return (r[:m, :n] + r[m:, :n]) + (r[:m, n:] + r[m:, n:])


def kernel(
    seg, lx, ly, width, owned, cb, n_line, n_tx, n_ty,
    rhs_ref, start_ref, inv_hbm, ls_ref, us_ref, low_ref, upp_ref, fb_ref, kind_ref, scale_ref, agg_ref,
    rm_ref, ci_ref,
    corr_ref, res_ref,
    inv_ref, invt_ref, q_ref, p_ref, ff_ref, f_ref, g_ref, h_ref,
    mask_ref, lu_ref, wf_ref, rmt_ref, rm4_ref, coef_ref, nb0_ref, nb1_ref, nb2_ref, nb3_ref,
    field_ref, diff_ref, base_ref,
    sx_ref, sy_ref, hx_ref, hy_ref, us_buf, ur_buf, ds_buf, dr_buf,
    abuf, cbuf, pbuf, oht_ref, ct_ref,
    inv_sem, hs_sem, hr_sem, uss_sem, usr_sem, dss_sem, dsr_sem, as_sem, ar_sem, cs_sem, cr_sem, ps_sem, pr_sem,
):
    lines = lx * ly
    rows = seg * lines
    line, tx, ty = lax.axis_index("line"), lax.axis_index("tx"), lax.axis_index("ty")
    has = (tx > 0, tx < n_tx - 1, ty > 0, ty < n_ty - 1)

    inv_copy = pltpu.make_async_copy(inv_hbm, inv_ref, inv_sem)
    inv_copy.start()

    def to_peer(o):
        return {"ty": lax.rem(ty + o, n_ty)}

    barrier = pltpu.get_barrier_semaphore()
    near = (
        (has[0], {"tx": tx - 1}), (has[1], {"tx": tx + 1}),
        (line > 0, {"line": line - 1}), (line < n_line - 1, {"line": line + 1}),
    )
    for there, device in near:
        @pl.when(there)
        def _(device=device):
            pl.semaphore_signal(barrier, inc=1, device_id=device, device_id_type=MESH)
    for o in range(1, n_ty):
        pl.semaphore_signal(barrier, inc=1, device_id=to_peer(o), device_id_type=MESH)

    def pack(source, turn):
        for i in range(seg):
            sx_ref[turn, 0, i * ly:(i + 1) * ly] = source[i * lines:i * lines + ly]
            sx_ref[turn, 1, i * ly:(i + 1) * ly] = source[(i + 1) * lines - ly:(i + 1) * lines]
        sy_ref[turn, 0] = source[pl.ds(0, seg * lx, stride=ly), :]
        sy_ref[turn, 1] = source[pl.ds(ly - 1, seg * lx, stride=ly), :]

    def remote(src, dst, ssem, rsem, device):
        return pltpu.make_async_remote_copy(
            src_ref=src, dst_ref=dst, send_sem=ssem, recv_sem=rsem, device_id=device, device_id_type=MESH
        )

    def halo(turn, side):
        send, land = (sx_ref, hx_ref) if side < 2 else (sy_ref, hy_ref)
        step = 1 if side % 2 else -1
        device = {"tx": tx + step} if side < 2 else {"ty": ty + step}
        other = side + 1 - 2 * (side % 2)
        return remote(
            send.at[turn, side % 2], land.at[turn, other % 2], hs_sem.at[turn, side], hr_sem.at[turn, other], device
        )

    def arriving(turn, side):
        send, land = (sx_ref, hx_ref) if side < 2 else (sy_ref, hy_ref)
        device = {"tx": tx} if side < 2 else {"ty": ty}
        return remote(
            send.at[turn, side % 2], land.at[turn, side % 2], hs_sem.at[turn, side], hr_sem.at[turn, side], device
        )

    def send_halos(turn):
        for side in (2, 3, 0, 1):
            @pl.when(has[side])
            def _(side=side):
                halo(turn, side).start()

    def wait_halos(turn):
        for side in (0, 1, 2, 3):
            @pl.when(has[side])
            def _(side=side):
                arriving(turn, side).wait_recv()

    field_ref[...] = start_ref[...]
    pack(field_ref, 0)
    for side in range(4):
        @pl.when(jnp.logical_not(has[side]))
        def _(side=side):
            land = hx_ref if side < 2 else hy_ref
            for turn in range(SWEEPS + 1):
                land[turn, side % 2] = jnp.zeros(land.shape[2:], F32)

    @pl.loop(0, rows, unroll=4)
    def _(e):
        i = lax.div(e, lines)
        l = lax.rem(e, lines)
        j = lax.div(l, ly)
        k = lax.rem(l, ly)
        for side in range(4):
            value = scale_ref[side, i, j, k]
            kind = kind_ref[side, i, j, k]
            for w in range(4):
                coef_ref[side * 4 + w, pl.ds(e, 1), :] = jnp.full(
                    (1, width), jnp.where(kind == w, value, 0.0), F32
                )
        abuf[0, pl.ds(e, 1), :] = jnp.full((1, width), agg_ref[i, j, k].astype(F32), F32)

    peers = n_ty - 1
    for there, _device in near:
        peers = peers + jnp.where(there, 1, 0)
    pl.semaphore_wait(barrier, peers)
    send_halos(0)

    rep = width // cb
    placed = jnp.zeros((width, width), F32)
    for a in range(rep):
        stacked = jnp.concatenate([ci_ref[t * rep + a] for t in range(rep)], axis=0)
        lane = lax.broadcasted_iota(jnp.int32, (cb, width), 1)
        place = lane == lax.broadcasted_iota(jnp.int32, (cb, width), 0) + a * cb
        place = jnp.where(place, 1.0, 0.0).astype(BF16)
        for half in split(stacked):
            placed = placed + dot(half, place)
    cbuf[0] = placed

    def agg_copy(o):
        return remote(abuf.at[0], abuf.at[o], as_sem.at[o], ar_sem.at[o], to_peer(o))

    def ci_copy(o):
        return remote(cbuf.at[0], cbuf.at[o], cs_sem.at[o], cr_sem.at[o], to_peer(o))

    def proj_copy(o):
        return remote(pbuf.at[0], pbuf.at[o], ps_sem.at[o], pr_sem.at[o], to_peer(o))

    for o in range(1, n_ty):
        agg_copy(o).start()
        ci_copy(o).start()

    row = lax.broadcasted_iota(jnp.int32, (2 * lines, width), 0)
    for l in range(lines):
        chosen = jnp.logical_or(row == l, row == l + lines)
        mask_ref[:, l * width:(l + 1) * width] = jnp.where(chosen, 1.0, 0.0).astype(BF16)
    eye = (
        lax.broadcasted_iota(jnp.int32, (width, width), 0) == lax.broadcasted_iota(jnp.int32, (width, width), 1)
    )
    lu_ref[0:width] = wide(low_ref[...].T)
    lu_ref[width:2 * width, :width] = jnp.where(eye, 1.0, 0.0).astype(BF16)
    lu_ref[width:2 * width, width:] = jnp.zeros((width, width), BF16)
    lu_ref[2 * width:3 * width] = wide(upp_ref[...].T)
    for w in range(4):
        wf_ref[w * width:(w + 1) * width] = wide(fb_ref[w].T)
    rm4 = jnp.concatenate([rm_ref[...]] * rep, axis=0)
    rm4_ref[...] = wide(rm4)
    rmt_ref[...] = wide(rm4.T)

    inv_copy.wait()

    def at(l):
        return pl.ds(pl.multiple_of(l * width, width), width)

    def folded(i, l, left):
        pair = jnp.concatenate([inv_ref[i, l], inv_ref[i, l + 1]], axis=0)
        pair = jnp.concatenate([pair, pair], axis=1)
        return lax.dot_general(left, pair, (((1,), (1,)), ((), ())), preferred_element_type=F32)

    def halves(r):
        return r[:, :width] + r[:, width:]

    def stacked_twice(w):
        return jnp.concatenate([w, w], axis=0)

    for i in range(seg):
        @pl.loop(0, lines // 2, unroll=2)
        def _(pair, i=i):
            r = folded(i, pair * 2, lu_ref[0:2 * width])
            for m in range(2):
                l = pair * 2 + m
                scale = ls_ref[i, lax.div(l, ly), lax.rem(l, ly)]
                q = scale * r[:width, m * width:(m + 1) * width]
                q_ref[i, at(l), :] = wide(q)
                if i == 0:
                    ff_ref[0, at(l), :] = -q
                invt_ref[i, at(l), :] = r[width:, m * width:(m + 1) * width].astype(BF16)

    def upper_maps():
        for i in range(seg):
            @pl.loop(0, lines // 2, unroll=2)
            def _(pair, i=i):
                r = folded(i, pair * 2, lu_ref[2 * width:3 * width])
                for m in range(2):
                    l = pair * 2 + m
                    scale = us_ref[i, lax.div(l, ly), lax.rem(l, ly)]
                    p = scale * r[:, m * width:(m + 1) * width]
                    p_ref[i, at(l), :] = wide(p)
                    if i == seg - 1:
                        h_ref[i, at(l), :] = wide(-p)

    def forward_maps():
        for i in range(1, seg):
            @pl.loop(0, lines, unroll=4)
            def _(l, i=i):
                f = -halves(dot(wide(ff_ref[i - 1, at(l), :]), stacked_twice(q_ref[i, at(l), :])))
                ff_ref[i, at(l), :] = f
                if i == seg - 1:
                    both = wide(f)
                    f_ref[at(l), :] = both
                    g_ref[i, at(l), :] = both

    def backward_maps():
        for i in range(seg - 2, -1, -1):
            @pl.loop(0, lines, unroll=4)
            def _(l, i=i):
                left = jnp.concatenate([g_ref[i + 1, at(l), :], h_ref[i + 1, at(l), :]], axis=0)
                r = halves(dot(left, stacked_twice(p_ref[i, at(l), :])))
                g_ref[i, at(l), :] = wide(ff_ref[i, at(l), :] - r[:width])
                h_ref[i, at(l), :] = wide(-r[width:])

    def spread(x):
        return jnp.concatenate([tall(x)] * lines, axis=1) * mask_ref[...]

    def apply(x, weights):
        return quadrants(dot(spread(x), weights))

    def coupled(v, turn):
        wait_halos(turn)
        nb0_ref[...] = pltpu.roll(v, ly, 0)
        nb1_ref[...] = pltpu.roll(v, rows - ly, 0)
        nb2_ref[...] = pltpu.roll(v, 1, 0)
        nb3_ref[...] = pltpu.roll(v, rows - 1, 0)
        for i in range(seg):
            nb0_ref[i * lines:i * lines + ly] = hx_ref[turn, 0, i * ly:(i + 1) * ly]
            nb1_ref[(i + 1) * lines - ly:(i + 1) * lines] = hx_ref[turn, 1, i * ly:(i + 1) * ly]
        nb2_ref[pl.ds(0, seg * lx, stride=ly), :] = hy_ref[turn, 0]
        nb3_ref[pl.ds(ly - 1, seg * lx, stride=ly), :] = hy_ref[turn, 1]
        beside = (nb0_ref[...], nb1_ref[...], nb2_ref[...], nb3_ref[...])
        left = []
        for w in range(4):
            total = coef_ref[w] * beside[0]
            for side in range(1, 4):
                total = total + coef_ref[side * 4 + w] * beside[side]
            left.append(tall(total))
        return quadrants(dot(jnp.concatenate(left, axis=1), wf_ref[...]))

    def up_copy(sweep):
        return remote(us_buf.at[sweep], ur_buf.at[sweep], uss_sem.at[sweep], usr_sem.at[sweep], {"line": line + 1})

    def down_copy(sweep):
        return remote(ds_buf.at[sweep], dr_buf.at[sweep], dss_sem.at[sweep], dsr_sem.at[sweep], {"line": line - 1})

    first, last = line == 0, line == n_line - 1
    late = line >= n_line // 2
    def from_above(sweep):
        @pl.when(jnp.logical_not(last))
        def _():
            down_copy(sweep).wait_recv()

        behind = spread(dr_buf[sweep])
        x = base_ref[0] + quadrants(dot(behind, h_ref[0]))

        @pl.when(jnp.logical_not(jnp.logical_or(first, last)))
        def _():
            ds_buf[sweep] = x
            down_copy(sweep).start()

        field_ref[0:lines] = x
        for i in range(1, seg):
            field_ref[i * lines:(i + 1) * lines] = base_ref[i] + quadrants(dot(behind, h_ref[i]))

    def early(sweep):
        drive = rhs_ref[...] - coupled(field_ref[...], sweep)
        for i in range(seg):
            r = dot(spread(drive[i * lines:(i + 1) * lines]), invt_ref[i])
            base_ref[i] = r[:lines] + r[lines:]

        @pl.when(late)
        def _():
            upper_maps()
            forward_maps()

        pl.when(last)(backward_maps)

        @pl.when(first)
        def _():
            ur_buf[sweep] = jnp.zeros((lines, width), F32)

        @pl.when(jnp.logical_not(first))
        def _():
            up_copy(sweep).wait_recv()

        y = ur_buf[sweep]
        for i in range(seg):
            y = base_ref[i] - apply(y, q_ref[i])
            base_ref[i] = y

        @pl.when(jnp.logical_not(last))
        def _():
            us_buf[sweep] = y
            up_copy(sweep).start()

        @pl.when(jnp.logical_not(late))
        def _():
            upper_maps()
            forward_maps()

        pl.when(jnp.logical_not(last))(backward_maps)

        b = base_ref[seg - 1]
        for i in range(seg - 2, -1, -1):
            b = base_ref[i] - apply(b, p_ref[i])
            base_ref[i] = b

        @pl.when(last)
        def _():
            ds_buf[sweep] = b
            dr_buf[sweep] = jnp.zeros((lines, width), F32)
            if n_line > 1:
                down_copy(sweep).start()

        from_above(sweep)

    def mapped(sweep):
        drive = rhs_ref[...] - coupled(field_ref[...], sweep)
        z = []
        for i in range(seg):
            r = dot(spread(drive[i * lines:(i + 1) * lines]), invt_ref[i])
            z.append(r[:lines] + r[lines:])
            if i > 0:
                z[i] = z[i] - apply(z[i - 1], q_ref[i])

        @pl.when(first)
        def _():
            us_buf[sweep] = z[seg - 1]
            ur_buf[sweep] = jnp.zeros((lines, width), F32)
            if n_line > 1:
                up_copy(sweep).start()

        w = [None] * seg
        w[seg - 1] = z[seg - 1]
        for i in range(seg - 2, -1, -1):
            w[i] = z[i] - apply(w[i + 1], p_ref[i])
        for i in range(seg):
            base_ref[i] = w[i]

        @pl.when(jnp.logical_not(first))
        def _():
            up_copy(sweep).wait_recv()

            @pl.when(jnp.logical_not(last))
            def _():
                us_buf[sweep] = z[seg - 1] + apply(ur_buf[sweep], f_ref[...])
                up_copy(sweep).start()

        incoming = spread(ur_buf[sweep])
        base = base_ref[0] + quadrants(dot(incoming, g_ref[0]))
        base_ref[0] = base

        @pl.when(last)
        def _():
            ds_buf[sweep] = base
            dr_buf[sweep] = jnp.zeros((lines, width), F32)
            if n_line > 1:
                down_copy(sweep).start()

        for i in range(1, seg):
            base_ref[i] = base_ref[i] + quadrants(dot(incoming, g_ref[i]))

        from_above(sweep)

    for sweep in range(SWEEPS):
        v = field_ref[...]
        (early if sweep == 0 else mapped)(sweep)
        if sweep < SWEEPS - 1:
            pack(field_ref, sweep + 1)
            send_halos(sweep + 1)
        else:
            diff_ref[...] = v - field_ref[...]
            pack(diff_ref, sweep + 1)
            send_halos(sweep + 1)

    aggs = oht_ref.shape[0]
    for o in range(1, n_ty):
        agg_copy(o).wait_recv()
        ci_copy(o).wait_recv()
    for o in range(n_ty):
        ids = abuf[o].T
        for b in range(aggs // width):
            index = lax.broadcasted_iota(jnp.int32, (width, rows), 0) + b * width
            oht_ref[b * width:(b + 1) * width, o * rows:(o + 1) * rows] = jnp.where(
                ids == index.astype(F32), 1.0, 0.0
            ).astype(BF16)
        ct_ref[:, 2 * o * width:2 * (o + 1) * width] = wide(cbuf[o].T)

    residual = coupled(diff_ref[...], SWEEPS)
    res_ref[...] = residual
    pbuf[0] = quadrants(dot(tall(residual), rmt_ref[...]))
    for o in range(1, n_ty):
        proj_copy(o).start()

    a_row = lax.broadcasted_iota(jnp.int32, (aggs, width), 0)
    group = lax.div(lax.broadcasted_iota(jnp.int32, (aggs, width), 1), cb)
    within = lax.rem(a_row, rep)
    own_ids = abuf[0]
    chosen = []
    for b in range(aggs // width):
        index = lax.broadcasted_iota(jnp.int32, (rows, width), 1) + b * width
        chosen.append(jnp.where(own_ids == index.astype(F32), 1.0, 0.0).astype(BF16))
    for o in range(1, n_ty):
        proj_copy(o).wait_recv()
    gathered = wide(pbuf[...].reshape(n_ty * rows, width))
    sums = dot(oht_ref[...], gathered)
    sums = sums[:, :width] + sums[:, width:]
    sums = jnp.where(group == within, sums, 0.0)
    images = dot(tall(sums), ct_ref[...])
    update = jnp.zeros((aggs, width), F32)
    for o in range(n_ty):
        part = quadrants(images[:, 2 * o * width:2 * (o + 1) * width])
        owner = lax.rem(ty + (n_ty - o), n_ty)
        update = update + jnp.where(owner * owned + group * rep + within == a_row, part, 0.0)
    fine = quadrants(dot(tall(update), rm4_ref[...]))
    r = dot(jnp.concatenate(chosen, axis=1), wide(fine))
    corr_ref[...] = field_ref[...] + (r[:, :width] + r[:, width:])

    for turn in range(SWEEPS + 1):
        for side in range(4):
            @pl.when(has[side])
            def _(turn=turn, side=side):
                halo(turn, side).wait_send()
    for sweep in range(SWEEPS):
        @pl.when(jnp.logical_not(last))
        def _(sweep=sweep):
            up_copy(sweep).wait_send()

        @pl.when(jnp.logical_not(first))
        def _(sweep=sweep):
            down_copy(sweep).wait_send()
    for o in range(1, n_ty):
        agg_copy(o).wait_send()
        ci_copy(o).wait_send()
        proj_copy(o).wait_send()


def body(
    right_side, start_field, line_inverse, lower_scale, upper_scale, lower_block, upper_block, face_blocks,
    face_kind, face_scale, agglomerate, restriction, coarse_inverse,
):
    seg, lx, ly, width = right_side.shape
    owned, cb = coarse_inverse.shape[2:4]
    lines = lx * ly
    rows = seg * lines
    n_line, n_tx, n_ty = (lax.axis_size(axis) for axis in ("line", "tx", "ty"))
    rep = width // cb
    groups = owned // rep
    assert rep * cb == width and groups == rep and groups * rep == owned
    aggs = -(-owned * n_ty // width) * width
    tall_k = lines * width
    vmem, smem = pl.BlockSpec(memory_space=pltpu.VMEM), pl.BlockSpec(memory_space=pltpu.SMEM)
    dma = pltpu.SemaphoreType.DMA
    turns = SWEEPS + 1
    scratch = [
        pltpu.VMEM((seg, lines, width, width), BF16),
        pltpu.VMEM((seg, tall_k, width), BF16),
        pltpu.VMEM((seg, tall_k, 2 * width), BF16),
        pltpu.VMEM((seg, tall_k, 2 * width), BF16),
        pltpu.VMEM((seg, tall_k, width), F32),
        pltpu.VMEM((tall_k, 2 * width), BF16),
        pltpu.VMEM((seg, tall_k, 2 * width), BF16),
        pltpu.VMEM((seg, tall_k, 2 * width), BF16),
        pltpu.VMEM((2 * lines, tall_k), BF16),
        pltpu.VMEM((3 * width, 2 * width), BF16),
        pltpu.VMEM((4 * width, 2 * width), BF16),
        pltpu.VMEM((width, 2 * width), BF16),
        pltpu.VMEM((width, 2 * width), BF16),
        pltpu.VMEM((16, rows, width), F32),
        pltpu.VMEM((rows, width), F32),
        pltpu.VMEM((rows, width), F32),
        pltpu.VMEM((rows, width), F32),
        pltpu.VMEM((rows, width), F32),
        pltpu.VMEM((rows, width), F32),
        pltpu.VMEM((rows, width), F32),
        pltpu.VMEM((seg, lines, width), F32),
        pltpu.VMEM((turns, 2, seg * ly, width), F32),
        pltpu.VMEM((turns, 2, seg * lx, width), F32),
        pltpu.VMEM((turns, 2, seg * ly, width), F32),
        pltpu.VMEM((turns, 2, seg * lx, width), F32),
        pltpu.VMEM((SWEEPS, lines, width), F32),
        pltpu.VMEM((SWEEPS, lines, width), F32),
        pltpu.VMEM((SWEEPS, lines, width), F32),
        pltpu.VMEM((SWEEPS, lines, width), F32),
        pltpu.VMEM((n_ty, rows, width), F32),
        pltpu.VMEM((n_ty, width, width), F32),
        pltpu.VMEM((n_ty, rows, width), F32),
        pltpu.VMEM((aggs, n_ty * rows), BF16),
        pltpu.VMEM((width, 2 * n_ty * width), BF16),
        dma, dma((turns, 4)), dma((turns, 4)),
        dma((SWEEPS,)), dma((SWEEPS,)), dma((SWEEPS,)), dma((SWEEPS,)),
        dma((n_ty,)), dma((n_ty,)), dma((n_ty,)), dma((n_ty,)), dma((n_ty,)), dma((n_ty,)),
    ]
    flat = jax.ShapeDtypeStruct((rows, width), F32)
    corrected, residual = pl.pallas_call(
        functools.partial(kernel, seg, lx, ly, width, owned, cb, n_line, n_tx, n_ty),
        out_shape=(flat, flat),
        in_specs=[
            vmem, vmem, pl.BlockSpec(memory_space=pl.ANY), smem, smem, vmem, vmem, vmem, smem, smem, smem, vmem, vmem,
        ],
        out_specs=(vmem, vmem),
        scratch_shapes=scratch,
        compiler_params=pltpu.CompilerParams(
            collective_id=0, has_side_effects=True, vmem_limit_bytes=60 * 2**20
        ),
    )(
        right_side.reshape(rows, width), start_field.reshape(rows, width),
        line_inverse.reshape(seg, lines, width, width), lower_scale, upper_scale, lower_block, upper_block,
        face_blocks, face_kind, face_scale, agglomerate, restriction,
        coarse_inverse.reshape(owned, cb, cb),
    )
    return corrected.reshape(right_side.shape), residual.reshape(right_side.shape)


def solution(mesh):
    in_specs = (
        P("line", "tx", "ty", None),
        P("line", "tx", "ty", None),
        P("line", "tx", "ty", None, None),
        P("line", "tx", "ty"),
        P("line", "tx", "ty"),
        P(),
        P(),
        P(),
        P(None, "line", "tx", "ty"),
        P(None, "line", "tx", "ty"),
        P("line", "tx", "ty"),
        P(),
        P("line", "tx", "ty", None, None),
    )
    out_specs = (P("line", "tx", "ty", None), P("line", "tx", "ty", None))
    return jax.shard_map(body, mesh=mesh, in_specs=in_specs, out_specs=out_specs, check_vma=False)
```
